32 devices in a mesh: node: 8 (over z, x), local: 4 (over y, core).
Axes of the slice: x: 2, y: 2, z: 4, core: 2. Of those that a mesh axis runs over, the one named last changes fastest.
Arguments:
- tokens: bfloat16 [4096, 2048], P(('node', 'local')), may hold values from -6 to 6
- expert_ids: int32 [4096, 6], P(('node', 'local')), may hold values from 0 to 15, all different within a row; in each aligned block of 128 rows (0 to 127, 128 to 255, ...) at most 82 rows name the same one
- gate_codes: int32 [4096, 6], P(('node', 'local')), may hold values from 1 to 1023
- gate_halves: bfloat16 [32, 2048, 704], P(('node', 'local')), may hold values from -0.125 to 0.125
- up_halves: bfloat16 [32, 2048, 704], P(('node', 'local')), may hold values from -0.125 to 0.125
- down_halves: bfloat16 [32, 1408, 1024], P(('node', 'local')), may hold values from -0.15625 to 0.15625
- shared_gate: bfloat16 [2048, 2816], P(None, 'local'), may hold values from -0.125 to 0.125
- shared_up: bfloat16 [2048, 2816], P(None, 'local'), may hold values from -0.125 to 0.125
- shared_down: bfloat16 [2816, 2048], P('local'), may hold values from -0.109375 to 0.109375
Outputs:
- mixed: bfloat16 [4096, 2048], P(('node', 'local'))
The draws below stay inside these ranges and needn't reach their ends.
Inputs may be any that keep to these rules, and one draw needn't show every extreme that they name: `expert_ids`: the experts of one token differ. Among the rows of one device, no expert is named more than 82 times, a bound that some block reaches; every expert is named somewhere.
All inputs are finite; a program needn't handle non-finite values.
Results may differ from the reference program's by a relative error of at most 0.01.
Values may be sent and summed in bfloat16 or wider, within the bound.
A program may use at most 128 MiB of HBM per device.

```python
import math
import jax
import jax.numpy as jnp
import numpy as np
from jax import lax

D = 2048
FF = 1408
SHARED = 2816
TOPK = 6
TOK_DEV = 128
EXPERTS = 16
CAP = 82
TOKENS = 4096
N_LOCAL = 4
DEVICES = 32


def with_ends(entries, stream_key, least, top_value):
    shape = entries.shape
    index_at = [jax.random.randint(jax.random.fold_in(stream_key, axis), (), 0, shape[axis]) for axis in range(len(shape))]
    entries = entries.at[tuple(index_at)].set(least)
    longest = shape.index(max(shape))
    index_at[longest] = (index_at[longest] + 1) % shape[longest]
    return entries.at[tuple(index_at)].set(top_value)


def block_levels(key, shape, cuts, smallest, largest):
    gain, own = 1.0, jax.random.fold_in(key, 6)
    for axis_at, blocks in cuts:
        steps = jnp.exp(jax.random.uniform(jax.random.fold_in(own, axis_at), (blocks,), jnp.float32, smallest / len(cuts), largest / len(cuts)))
        gain = gain * jnp.repeat(steps, shape[axis_at] // blocks).reshape([-1 if axis == axis_at else 1 for axis in range(len(shape))])
    return gain


def routed_block(stream_key, own, number, rows, count, top, limit, slope):
    order = jax.random.permutation(stream_key, count)
    heavy_load, common = portions_of(count, rows * top, limit, slope, True), portions_of(count, rows * top, limit, slope, False)
    places = jnp.arange(count)

    def named(tallies, rotation):
        used = int((tallies > 0).sum())
        fixed = max(1, used // 4)
        shifted = fixed + (places - fixed + rotation * (used - fixed)) % max(1, count - fixed)
        return jnp.zeros((count,), jnp.int32).at[order[jnp.where(places < fixed, places, shifted)]].set(jnp.asarray(tallies, jnp.int32))

    tallies = jnp.where(number % 4 == 0, named(heavy_load, number // 4), named(common, number - number // 4 - 1))
    mixed = jax.random.permutation(jax.random.fold_in(own, 3), count)
    source_of, taker = mixed[0:count // 2 * 2:2], mixed[1:count // 2 * 2:2]
    margin = jnp.minimum(tallies[source_of] - 1, limit - tallies[taker]) // 2
    margin = jnp.where((source_of == order[0]) | (taker == order[0]) | (tallies[taker] == 0), 0, jnp.maximum(margin, 0))
    shifted = jax.random.randint(jax.random.fold_in(own, 4), (count // 2,), 0, 1 << 20) % (margin + 1)
    tallies = tallies.at[source_of].add(-shifted).at[taker].add(shifted)
    labels = jnp.searchsorted(jnp.cumsum(tallies), jnp.arange(rows * top), side="right").astype(jnp.int32)
    listing = labels.reshape(top, rows).T
    listing = listing[jax.random.permutation(jax.random.fold_in(own, 1), rows)]
    rotation = jax.random.randint(jax.random.fold_in(own, 2), (rows, 1), 0, top)
    return jnp.take_along_axis(listing, (jnp.arange(top)[None, :] + rotation) % top, axis=1)


def portions_of(number_of, total, reach, lean, full):
    loads = [(1 << 20) // math.isqrt(standing ** lean) + 1 for standing in range(1, number_of + 1)]
    largest = reach if full else min(reach, max(-(-total // number_of), total * loads[0] // sum(loads)))
    least = 1 if total - largest >= number_of - 1 else 0
    holding, surplus = [largest] + [least] * (number_of - 1), total - largest - least * (number_of - 1)
    while surplus > 0:
        free = [i for i in range(1, number_of) if holding[i] < largest] or [i for i in range(1, number_of) if holding[i] < reach]
        pool, remaining = sum([loads[i] for i in free]), surplus
        for i in free:
            more = min(reach - holding[i], max(1, remaining * loads[i] // pool), surplus)
            holding[i] = holding[i] + more
            surplus = surplus - more
    return np.array(holding)


def gaussian(rng, shape, deviation, reach, split=(), kind=jnp.bfloat16):
    values = deviation * jax.random.normal(rng, shape, jnp.float32)
    if split:
        values = values * block_levels(rng, shape, split, -0.22, 0.18)
    return jnp.clip(values, -reach, reach).astype(kind)


def setup_inputs(seed: int = 0) -> dict:
    key_list = jax.random.split(jax.random.key(seed), 10)
    tokens = gaussian(key_list[0], (TOKENS, D), 1.0, 6.0, ((0, 32),))
    expert_ids_keys = jax.random.split(jax.random.fold_in(key_list[1], 1), TOKENS // TOK_DEV)
    expert_ids_turns = jax.random.permutation(jax.random.fold_in(key_list[1], 3), TOKENS // TOK_DEV)
    expert_ids = jax.vmap(lambda own, number: routed_block(jax.random.fold_in(key_list[1], 2), own, number, TOK_DEV, EXPERTS, TOPK, CAP, 2))(expert_ids_keys, expert_ids_turns).reshape((TOKENS, TOPK))
    gate_codes = with_ends(jax.random.randint(key_list[2], (TOKENS, TOPK), 1, 1024), jax.random.fold_in(key_list[2], 1), 1, 1023).astype(jnp.int32)
    gate_halves = gaussian(key_list[3], (2 * EXPERTS, D, FF // 2), D ** -0.5, 0.125, ((0, 32),))
    up_halves = gaussian(key_list[4], (2 * EXPERTS, D, FF // 2), D ** -0.5, 0.125, ((0, 32),))
    down_halves = gaussian(key_list[5], (2 * EXPERTS, FF, D // 2), FF ** -0.5, 0.15625, ((0, 32),))
    shared_gate = gaussian(key_list[6], (D, SHARED), D ** -0.5, 0.125, ((1, 4),))
    shared_up = gaussian(key_list[7], (D, SHARED), D ** -0.5, 0.125, ((1, 4),))
    shared_down = gaussian(key_list[8], (SHARED, D), SHARED ** -0.5, 0.109375, ((0, 4),))
    return {"tokens": tokens, "expert_ids": expert_ids, "gate_codes": gate_codes, "gate_halves": gate_halves, "up_halves": up_halves, "down_halves": down_halves, "shared_gate": shared_gate, "shared_up": shared_up, "shared_down": shared_down}


def reference(tokens, expert_ids, gate_codes, gate_halves, up_halves, down_halves, shared_gate, shared_up, shared_down):
    features = tokens.shape[1]
    route_ids = expert_ids.reshape(DEVICES, TOK_DEV * TOPK).astype(jnp.int32)
    onehot = (route_ids[:, :, None] == jnp.arange(EXPERTS, dtype=jnp.int32)[None, None, :]).astype(jnp.int32)
    slot_index = jnp.sum((jnp.cumsum(onehot, axis=1) - 1) * onehot, axis=2).astype(jnp.int32)
    source_rows = jnp.arange(DEVICES, dtype=jnp.int32)[:, None]
    slot_column = (source_rows * CAP + slot_index).astype(jnp.int32)
    owner_row = (jnp.arange(DEVICES * TOK_DEV * TOPK, dtype=jnp.int32) // TOPK).astype(jnp.int32).reshape(DEVICES, TOK_DEV * TOPK)
    codes = gate_codes.astype(jnp.float32)
    weights = (codes / jnp.sum(codes, axis=1, keepdims=True)).reshape(DEVICES, TOK_DEV * TOPK)
    token_table = jnp.full((EXPERTS, DEVICES * CAP), TOKENS, jnp.int32).at[route_ids, slot_column].set(owner_row)
    weight_table = jnp.zeros((EXPERTS, DEVICES * CAP), jnp.float32).at[route_ids, slot_column].set(weights)
    padded = jnp.concatenate([tokens, jnp.zeros((1, features), tokens.dtype)], axis=0)

    def add_expert(running, expert):
        rows_index = token_table[expert]
        expert_rows = padded[rows_index]
        gate_full = jnp.concatenate([gate_halves[2 * expert], gate_halves[2 * expert + 1]], axis=1)
        up_full = jnp.concatenate([up_halves[2 * expert], up_halves[2 * expert + 1]], axis=1)
        down_full = jnp.concatenate([down_halves[2 * expert], down_halves[2 * expert + 1]], axis=1)
        gate_out = jnp.dot(expert_rows, gate_full, preferred_element_type=jnp.float32)
        up_out = jnp.dot(expert_rows, up_full, preferred_element_type=jnp.float32)
        hidden = (jax.nn.silu(gate_out) * up_out).astype(tokens.dtype)
        result = jnp.dot(hidden, down_full, preferred_element_type=jnp.float32).astype(tokens.dtype)
        running = running.at[rows_index].add(result.astype(jnp.float32) * weight_table[expert][:, None])
        return running, None

    routed, unused = lax.scan(add_expert, jnp.zeros((TOKENS + 1, features), jnp.float32), jnp.arange(EXPERTS, dtype=jnp.int32))
    shared_hidden = (jax.nn.silu(jnp.dot(tokens, shared_gate, preferred_element_type=jnp.float32)) * jnp.dot(tokens, shared_up, preferred_element_type=jnp.float32)).astype(tokens.dtype)
    slice_width = SHARED // N_LOCAL
    shared_out = jnp.zeros((TOKENS, features), jnp.float32)
    for column in range(N_LOCAL):
        partial_sum = jnp.dot(shared_hidden[:, column * slice_width:(column + 1) * slice_width], shared_down[column * slice_width:(column + 1) * slice_width], preferred_element_type=jnp.float32)
        shared_out = shared_out + partial_sum.astype(tokens.dtype).astype(jnp.float32)
    return (routed[:TOKENS] + shared_out).astype(tokens.dtype)
```

```python
import jax
import jax.numpy as jnp
from jax import lax
from jax.sharding import PartitionSpec as P


def from_partner(block, axis, distance):
    count = lax.axis_size(axis)
    route = []
    for low in range(count):
        high = low | 1 << distance
        if high != low and high < count:
            route += [(low, high), (high, low)]
    return lax.ppermute(block, axis, route)


def dispatch(send_block):
    return lax.all_to_all(send_block, ("node", "local"), split_axis=0, concat_axis=0, tiled=True)


def combine(send_block):
    return lax.all_to_all(send_block, ("node", "local"), split_axis=0, concat_axis=0, tiled=True)


def half_hidden(received, gate_half, up_half, dtype):
    expert_rows = received.reshape(-1, received.shape[-1])
    gate_out = jnp.dot(expert_rows, gate_half, preferred_element_type=jnp.float32)
    up_out = jnp.dot(expert_rows, up_half, preferred_element_type=jnp.float32)
    return (jax.nn.silu(gate_out) * up_out).astype(dtype)


def side_by_side(own_part, other_part, parity, axis):
    lower = jnp.where(parity == 0, own_part, other_part)
    upper = jnp.where(parity == 0, other_part, own_part)
    return jnp.concatenate([lower, upper], axis=axis)


def local(
    tokens,
    expert_ids,
    gate_codes,
    gate_halves,
    up_halves,
    down_halves,
    shared_gate,
    shared_up,
    shared_down,
):
    tok_rows, features = tokens.shape
    fanout = expert_ids.shape[1]
    devices = lax.axis_size("node") * lax.axis_size("local")
    experts = devices // 2
    capacity = 2 * (5 * tok_rows * fanout // (6 * experts) + 1)
    parity = lax.axis_index("local") % 2
    flat_ids = expert_ids.reshape(-1)
    onehot = (flat_ids[:, None] == jnp.arange(experts, dtype=jnp.int32)[None, :]).astype(jnp.int32)
    slot_index = jnp.sum((jnp.cumsum(onehot, axis=0) - 1) * onehot, axis=1)
    dest_row = flat_ids * capacity + slot_index
    owner_row = jnp.arange(tok_rows * fanout, dtype=jnp.int32) // fanout
    buffer = (
        jnp.zeros((experts * capacity, features), tokens.dtype).at[dest_row].set(tokens[owner_row])
    )
    codes = gate_codes.astype(jnp.float32)
    weights = (codes / jnp.sum(codes, axis=1, keepdims=True)).reshape(-1)
    send_block = jnp.broadcast_to(
        buffer.reshape(experts, 1, capacity, features), (experts, 2, capacity, features)
    ).reshape(devices, capacity, features)
    received = dispatch(send_block)
    hidden_own = half_hidden(received, gate_halves[0], up_halves[0], tokens.dtype)
    hidden_other = from_partner(hidden_own, "local", 0)
    hidden = side_by_side(hidden_own, hidden_other, parity, 1)
    result = jnp.dot(hidden, down_halves[0], preferred_element_type=jnp.float32).astype(
        tokens.dtype
    )
    returned = combine(result.reshape(devices, capacity, features // 2))
    outputs = (
        returned.reshape(experts, 2, capacity, features // 2)
        .transpose(0, 2, 1, 3)
        .reshape(experts * capacity, features)
    )
    picked = outputs[dest_row].astype(jnp.float32) * weights[:, None]
    routed = jnp.sum(picked.reshape(tok_rows, fanout, features), axis=1)
    block_rows = lax.all_gather(tokens, "local", axis=0, tiled=True)
    gate_part = jnp.dot(block_rows, shared_gate, preferred_element_type=jnp.float32)
    up_part = jnp.dot(block_rows, shared_up, preferred_element_type=jnp.float32)
    shared_hidden = (jax.nn.silu(gate_part) * up_part).astype(tokens.dtype)
    block_rows = shared_hidden
    shared_out = lax.psum_scatter(
        jnp.dot(block_rows, shared_down, preferred_element_type=jnp.float32).astype(jnp.bfloat16),
        "local",
        scatter_dimension=0,
        tiled=True,
    ).astype(jnp.float32)
    return (routed + shared_out).astype(tokens.dtype)

def swap_cores(block):
    return lax.ppermute(block, "core", [(0, 1), (1, 0)])


def both_halves(block, core):
    other = swap_cores(block)
    return jnp.where(core == 0, block, other), jnp.where(core == 0, other, block)


def dense(
    tokens,
    expert_ids,
    gate_codes,
    gate_halves,
    up_halves,
    down_halves,
    shared_gate,
    shared_up,
    shared_down,
):
    rows, features = tokens.shape
    planes = ("node", "chip")
    chips = lax.axis_size("node") * lax.axis_size("chip")
    group_chips = lax.axis_size("chip")
    core = lax.axis_index("core")
    chip = lax.axis_index("chip")
    node = lax.axis_index("node")
    expert = node * group_chips + chip

    codes = gate_codes.astype(jnp.float32)
    weights = codes / jnp.sum(codes, axis=1, keepdims=True)
    onehot = expert_ids[:, :, None] == jnp.arange(chips, dtype=jnp.int32)[None, None, :]
    table = jnp.sum(jnp.where(onehot, weights[:, :, None], 0.0), axis=1)

    plane_rows = lax.all_gather(tokens, planes, axis=0, tiled=True)
    share = lax.all_to_all(table.T.reshape(chips, 1, rows), planes, split_axis=0, concat_axis=0, tiled=True)
    scale = share.reshape(-1, 1)

    gate = both_halves(gate_halves[0], core)
    up = both_halves(up_halves[0], core)
    down = both_halves(down_halves[0], core)

    group = lax.all_gather(lax.all_gather(tokens, "chip", axis=0, tiled=True), "core", axis=0, tiled=True)
    shared_hidden = (
        jax.nn.silu(jnp.dot(group, shared_gate, preferred_element_type=jnp.float32))
        * jnp.dot(group, shared_up, preferred_element_type=jnp.float32)
    ).astype(tokens.dtype)
    shared_rows = jnp.dot(shared_hidden, shared_down, preferred_element_type=jnp.float32)
    shared_rows = shared_rows.astype(tokens.dtype).reshape(2, group_chips * rows, features)
    mine = jnp.where(core == 0, shared_rows[0], shared_rows[1])
    theirs = jnp.where(core == 0, shared_rows[1], shared_rows[0])
    shared_part = mine.astype(jnp.float32) + swap_cores(theirs).astype(jnp.float32)

    hidden = jnp.concatenate(
        [
            (
                jax.nn.silu(jnp.dot(plane_rows, gate[h], preferred_element_type=jnp.float32))
                * jnp.dot(plane_rows, up[h], preferred_element_type=jnp.float32)
            ).astype(tokens.dtype)
            for h in (0, 1)
        ],
        axis=1,
    )
    out = jnp.concatenate(
        [
            (jnp.dot(hidden, down[h], preferred_element_type=jnp.float32) * scale).astype(tokens.dtype)
            for h in (0, 1)
        ],
        axis=1,
    )
    first = node * group_chips * rows
    block = lax.dynamic_slice(out, (first, 0), (group_chips * rows, features))
    block = (block.astype(jnp.float32) + shared_part).astype(tokens.dtype)
    out = lax.dynamic_update_slice(out, block, (first, 0))
    return lax.psum_scatter(out, planes, scatter_dimension=0, tiled=True)


def program(mesh, row, pieces, body):
    in_specs = (
        P(row, None),
        P(row, None),
        P(row, None),
        P(row, None, None),
        P(row, None, None),
        P(row, None, None),
        P(None, pieces),
        P(None, pieces),
        P(pieces, None),
    )
    return jax.shard_map(
        body, mesh=mesh, in_specs=in_specs, out_specs=P(row, None), check_vma=False
    )


def solution(mesh):
    experts = mesh.devices.size // 2
    fine = jax.sharding.Mesh(
        mesh.devices.reshape(mesh.devices.shape[0], -1, 2), ("node", "chip", "core")
    )

    def run(tokens, expert_ids, *others):
        if experts <= 4 * expert_ids.shape[1]:
            whole = program(fine, ("node", "chip", "core"), ("chip", "core"), dense)
        else:
            whole = program(mesh, ("node", "local"), "local", local)
        return whole(tokens, expert_ids, *others)

    return run
```

```python
import functools

import jax
import jax.numpy as jnp
from jax import lax
from jax.experimental import pallas as pl
from jax.experimental.pallas import tpu as pltpu
from jax.sharding import PartitionSpec as P

MESH = pl.DeviceIdType.MESH


def from_partner(block, axis, distance):
    count = lax.axis_size(axis)
    route = []
    for low in range(count):
        high = low | 1 << distance
        if high != low and high < count:
            route += [(low, high), (high, low)]
    return lax.ppermute(block, axis, route)


def dispatch(send_block):
    return lax.all_to_all(send_block, ("node", "local"), split_axis=0, concat_axis=0, tiled=True)


def combine(send_block):
    return lax.all_to_all(send_block, ("node", "local"), split_axis=0, concat_axis=0, tiled=True)


def half_hidden(received, gate_half, up_half, dtype):
    expert_rows = received.reshape(-1, received.shape[-1])
    gate_out = jnp.dot(expert_rows, gate_half, preferred_element_type=jnp.float32)
    up_out = jnp.dot(expert_rows, up_half, preferred_element_type=jnp.float32)
    return (jax.nn.silu(gate_out) * up_out).astype(dtype)


def side_by_side(own_part, other_part, parity, axis):
    lower = jnp.where(parity == 0, own_part, other_part)
    upper = jnp.where(parity == 0, other_part, own_part)
    return jnp.concatenate([lower, upper], axis=axis)


def local(
    tokens,
    expert_ids,
    gate_codes,
    gate_halves,
    up_halves,
    down_halves,
    shared_gate,
    shared_up,
    shared_down,
):
    tok_rows, features = tokens.shape
    fanout = expert_ids.shape[1]
    devices = lax.axis_size("node") * lax.axis_size("local")
    experts = devices // 2
    capacity = 2 * (5 * tok_rows * fanout // (6 * experts) + 1)
    parity = lax.axis_index("local") % 2
    flat_ids = expert_ids.reshape(-1)
    onehot = (flat_ids[:, None] == jnp.arange(experts, dtype=jnp.int32)[None, :]).astype(jnp.int32)
    slot_index = jnp.sum((jnp.cumsum(onehot, axis=0) - 1) * onehot, axis=1)
    dest_row = flat_ids * capacity + slot_index
    owner_row = jnp.arange(tok_rows * fanout, dtype=jnp.int32) // fanout
    buffer = (
        jnp.zeros((experts * capacity, features), tokens.dtype).at[dest_row].set(tokens[owner_row])
    )
    codes = gate_codes.astype(jnp.float32)
    weights = (codes / jnp.sum(codes, axis=1, keepdims=True)).reshape(-1)
    send_block = jnp.broadcast_to(
        buffer.reshape(experts, 1, capacity, features), (experts, 2, capacity, features)
    ).reshape(devices, capacity, features)
    received = dispatch(send_block)
    hidden_own = half_hidden(received, gate_halves[0], up_halves[0], tokens.dtype)
    hidden_other = from_partner(hidden_own, "local", 0)
    hidden = side_by_side(hidden_own, hidden_other, parity, 1)
    result = jnp.dot(hidden, down_halves[0], preferred_element_type=jnp.float32).astype(
        tokens.dtype
    )
    returned = combine(result.reshape(devices, capacity, features // 2))
    outputs = (
        returned.reshape(experts, 2, capacity, features // 2)
        .transpose(0, 2, 1, 3)
        .reshape(experts * capacity, features)
    )
    picked = outputs[dest_row].astype(jnp.float32) * weights[:, None]
    routed = jnp.sum(picked.reshape(tok_rows, fanout, features), axis=1)
    block_rows = lax.all_gather(tokens, "local", axis=0, tiled=True)
    gate_part = jnp.dot(block_rows, shared_gate, preferred_element_type=jnp.float32)
    up_part = jnp.dot(block_rows, shared_up, preferred_element_type=jnp.float32)
    shared_hidden = (jax.nn.silu(gate_part) * up_part).astype(tokens.dtype)
    block_rows = shared_hidden
    shared_out = lax.psum_scatter(
        jnp.dot(block_rows, shared_down, preferred_element_type=jnp.float32).astype(jnp.bfloat16),
        "local",
        scatter_dimension=0,
        tiled=True,
    ).astype(jnp.float32)
    return (routed + shared_out).astype(tokens.dtype)


def place():
    node, chip, core = lax.axis_index("node"), lax.axis_index("chip"), lax.axis_index("core")
    return node // 2, node % 2, chip, core


def near(z, x, y, core, first):
    along_x = 1 - core if first else core
    return (z * 2 + x + along_x * (1 - 2 * x), y + (1 - along_x) * (1 - 2 * y), core)


def slot_of(z, x, y, core, p_other, q_other):
    x_other = p_other * (1 - core) + q_other * core
    y_other = p_other * core + q_other * (1 - core)
    return z * 4 + (x + x_other * (1 - 2 * x)) * 2 + y + y_other * (1 - 2 * y)


def greet(devices):
    barrier = pltpu.get_barrier_semaphore()
    for device in devices:
        pl.semaphore_signal(barrier, inc=1, device_id=device, device_id_type=MESH)
    pl.semaphore_wait(barrier, len(devices))


def gather_kernel(line, parts, *refs):
    tokens = refs[0]
    weights = refs[1 : 1 + parts]
    gathered = refs[1 + parts]
    both = refs[2 + parts : 2 + 2 * parts]
    own_sem, send_sem, recv_sem, keep_sem, weight_send, weight_recv = refs[2 + 2 * parts :]
    z, x, y, core = place()
    p_device, q_device = near(z, x, y, core, True), near(z, x, y, core, False)
    partner = (z * 2 + x, y, 1 - core)
    lines = [(lax.rem(z + d, line) * 2 + x, y, core) for d in range(1, line)]
    greet(lines + [p_device, q_device, partner])
    me = slot_of(z, x, y, core, 0, 0)

    def push(source, slot, count, device):
        copy = pltpu.make_async_remote_copy(
            src_ref=source,
            dst_ref=gathered.at[slot],
            send_sem=send_sem.at[count],
            recv_sem=recv_sem.at[slot],
            device_id=device,
            device_id_type=MESH,
        )
        copy.start()
        return copy

    def arrived(slot):
        pltpu.make_async_remote_copy(
            src_ref=gathered.at[slot],
            dst_ref=gathered.at[slot],
            send_sem=send_sem.at[0],
            recv_sem=recv_sem.at[slot],
            device_id=q_device,
            device_id_type=MESH,
        ).wait_recv()

    sent = []
    sent.append(push(tokens, me, len(sent), q_device))
    for device in lines:
        sent.append(push(tokens, me, len(sent), device))
    sent.append(push(tokens, me, len(sent), p_device))
    own = pltpu.make_async_copy(tokens, gathered.at[me], own_sem)
    own.start()
    moved, kept = [], []
    for at in range(parts):
        copy = pltpu.make_async_remote_copy(
            src_ref=weights[at],
            dst_ref=both[at].at[core],
            send_sem=weight_send.at[at],
            recv_sem=weight_recv.at[at],
            device_id=partner,
            device_id_type=MESH,
        )
        copy.start()
        moved.append(copy)
        keep = pltpu.make_async_copy(weights[at], both[at].at[core], keep_sem.at[at])
        keep.start()
        kept.append(keep)
    for d in [*range(1, line, 2), *range(2, line, 2)]:
        slot = slot_of(lax.rem(z + d, line), x, y, core, 0, 0)
        arrived(slot)
        sent.append(push(gathered.at[slot], slot, len(sent), q_device))
        sent.append(push(gathered.at[slot], slot, len(sent), p_device))
    for d in [0, *range(1, line, 2), *range(2, line, 2)]:
        slot = slot_of(lax.rem(z + d, line), x, y, core, 1, 0)
        arrived(slot)
        sent.append(push(gathered.at[slot], slot, len(sent), q_device))
    for p_other in (0, 1):
        for d in range(line):
            arrived(slot_of(lax.rem(z + d, line), x, y, core, p_other, 1))
    for copy in sent:
        copy.wait_send()
    own.wait()
    for at in range(parts):
        moved[at].wait()
        kept[at].wait()


def gather_plane(tokens, weights):
    chips = lax.axis_size("node") * lax.axis_size("chip")
    parts = len(weights)
    anywhere = pl.BlockSpec(memory_space=pl.ANY)
    shapes = [jax.ShapeDtypeStruct((chips, *tokens.shape), tokens.dtype)]
    shapes += [jax.ShapeDtypeStruct((2, *w.shape), w.dtype) for w in weights]
    return pl.pallas_call(
        functools.partial(gather_kernel, chips // 4, parts),
        out_shape=shapes,
        in_specs=[anywhere] * (1 + parts),
        out_specs=[anywhere] * (1 + parts),
        scratch_shapes=[
            pltpu.SemaphoreType.DMA,
            pltpu.SemaphoreType.DMA((chips - 1,)),
            pltpu.SemaphoreType.DMA((chips,)),
            pltpu.SemaphoreType.DMA((parts,)),
            pltpu.SemaphoreType.DMA((parts,)),
            pltpu.SemaphoreType.DMA((parts,)),
        ],
        compiler_params=pltpu.CompilerParams(collective_id=0, has_side_effects=True),
    )(tokens, *weights)


def reduce_kernel(line, terms, out, held, from_q, from_p, from_z, send_sem, q_sem, p_sem, z_sem):
    z, x, y, core = place()
    p_device, q_device = near(z, x, y, core, True), near(z, x, y, core, False)
    lines = [(lax.rem(z + d, line) * 2 + x, y, core) for d in range(1, line)]
    greet(lines + [p_device, q_device])
    turn = [*range(1, line), 0]

    def push(source, target, sem, count, device):
        copy = pltpu.make_async_remote_copy(
            src_ref=source,
            dst_ref=target,
            send_sem=send_sem.at[count],
            recv_sem=sem,
            device_id=device,
            device_id_type=MESH,
        )
        copy.start()
        return copy

    def add_up(target, sources):
        def step(i, carry):
            rows = pl.ds(pl.multiple_of(i * 16, 16), 16)
            total = sources[0][rows, :].astype(jnp.float32)
            for source in sources[1:]:
                total = total + source[rows, :].astype(jnp.float32)
            target[rows, :] = total.astype(target.dtype)
            return carry

        lax.fori_loop(0, out.shape[0] // 16, step, 0)

    sent, q_copies, p_copies, z_copies = [], {}, {}, {}
    for p_other in (1, 0):
        for d in turn:
            slot = slot_of(lax.rem(z + d, line), x, y, core, p_other, 1)
            at = p_other * line + d
            copy = push(terms.at[slot], from_q.at[at], q_sem.at[at], len(sent), q_device)
            sent.append(copy)
            q_copies[p_other, d] = copy
    for d in turn:
        at = line + d
        slot = slot_of(lax.rem(z + d, line), x, y, core, 1, 0)
        q_copies[1, d].wait_recv()
        add_up(held.at[at], [terms.at[slot], from_q.at[at]])
        p_copies[d] = push(held.at[at], from_p.at[d], p_sem.at[d], len(sent), p_device)
        sent.append(p_copies[d])
    for d in turn:
        slot = slot_of(lax.rem(z + d, line), x, y, core, 0, 0)
        q_copies[0, d].wait_recv()
        p_copies[d].wait_recv()
        sources = [terms.at[slot], from_q.at[d], from_p.at[d]]
        if d:
            add_up(held.at[d], sources)
            z_copies[d] = push(
                held.at[d], from_z.at[d - 1], z_sem.at[d - 1], len(sent), lines[d - 1]
            )
            sent.append(z_copies[d])
        else:
            for other in range(1, line):
                z_copies[other].wait_recv()
            add_up(out, sources + [from_z.at[other - 1] for other in range(1, line)])
    for copy in sent:
        copy.wait_send()


def reduce_plane(terms):
    chips, rows, features = terms.shape
    line = chips // 4
    inside = pl.BlockSpec(memory_space=pltpu.VMEM)
    return pl.pallas_call(
        functools.partial(reduce_kernel, line),
        out_shape=jax.ShapeDtypeStruct((rows, features), terms.dtype),
        in_specs=[inside],
        out_specs=inside,
        scratch_shapes=[
            pltpu.VMEM((2 * line, rows, features), terms.dtype),
            pltpu.VMEM((2 * line, rows, features), terms.dtype),
            pltpu.VMEM((line, rows, features), terms.dtype),
            pltpu.VMEM((line - 1, rows, features), terms.dtype),
            pltpu.SemaphoreType.DMA((chips - 1,)),
            pltpu.SemaphoreType.DMA((2 * line,)),
            pltpu.SemaphoreType.DMA((line,)),
            pltpu.SemaphoreType.DMA((line - 1,)),
        ],
        compiler_params=pltpu.CompilerParams(
            collective_id=1, has_side_effects=True, vmem_limit_bytes=40 << 20
        ),
    )(terms)


def gated(rows, gate, up):
    gate_out = jnp.dot(rows, gate, preferred_element_type=jnp.float32)
    up_out = jnp.dot(rows, up, preferred_element_type=jnp.float32)
    return (jax.nn.silu(gate_out) * up_out).astype(rows.dtype)


def dense(
    tokens,
    expert_ids,
    gate_codes,
    gate_halves,
    up_halves,
    down_halves,
    shared_gate,
    shared_up,
    shared_down,
):
    rows, features = tokens.shape
    planes = ("node", "chip")
    chips = lax.axis_size("node") * lax.axis_size("chip")
    group_rows = lax.axis_size("chip") * rows
    first = lax.axis_index("node") * group_rows

    codes = gate_codes.astype(jnp.float32)
    weights = codes / jnp.sum(codes, axis=1, keepdims=True)
    onehot = expert_ids[:, :, None] == jnp.arange(chips, dtype=jnp.int32)[None, None, :]
    table = jnp.sum(jnp.where(onehot, weights[:, :, None], 0.0), axis=1)
    share = lax.all_to_all(
        table.T.reshape(chips, 1, rows), planes, split_axis=0, concat_axis=0, tiled=True
    )
    scale = share.reshape(-1, 1)

    plane_rows, gate, up, down, s_gate, s_up, s_down = gather_plane(
        tokens,
        (gate_halves[0], up_halves[0], down_halves[0], shared_gate, shared_up, shared_down),
    )
    plane_rows = plane_rows.reshape(chips * rows, features)

    group = lax.dynamic_slice(plane_rows, (first, 0), (group_rows, features))
    shared_part = sum(
        jnp.dot(gated(group, s_gate[h], s_up[h]), s_down[h], preferred_element_type=jnp.float32)
        .astype(tokens.dtype)
        .astype(jnp.float32)
        for h in (0, 1)
    )
    hidden = jnp.concatenate([gated(plane_rows, gate[h], up[h]) for h in (0, 1)], axis=1)
    out = jnp.concatenate(
        [
            (jnp.dot(hidden, down[h], preferred_element_type=jnp.float32) * scale).astype(tokens.dtype)
            for h in (0, 1)
        ],
        axis=1,
    )
    block = lax.dynamic_slice(out, (first, 0), (group_rows, features))
    block = (block.astype(jnp.float32) + shared_part).astype(tokens.dtype)
    out = lax.dynamic_update_slice(out, block, (first, 0))
    return reduce_plane(out.reshape(chips, rows, features))


def program(mesh, row, pieces, body):
    in_specs = (
        P(row, None),
        P(row, None),
        P(row, None),
        P(row, None, None),
        P(row, None, None),
        P(row, None, None),
        P(None, pieces),
        P(None, pieces),
        P(pieces, None),
    )
    return jax.shard_map(
        body, mesh=mesh, in_specs=in_specs, out_specs=P(row, None), check_vma=False
    )


def solution(mesh):
    experts = mesh.devices.size // 2
    fine = jax.sharding.Mesh(
        mesh.devices.reshape(mesh.devices.shape[0], -1, 2), ("node", "chip", "core")
    )

    def run(tokens, expert_ids, *others):
        if mesh.shape["local"] == 4 and experts <= 4 * expert_ids.shape[1]:
            whole = program(fine, ("node", "chip", "core"), ("chip", "core"), dense)
        else:
            whole = program(mesh, ("node", "local"), "local", local)
        return whole(tokens, expert_ids, *others)

    return run
```

```python
import functools

import jax
import jax.numpy as jnp
from jax import lax
from jax.experimental import pallas as pl
from jax.experimental.pallas import tpu as pltpu
from jax.sharding import PartitionSpec as P

MESH = pl.DeviceIdType.MESH
NT = (((1,), (1,)), ((), ()))


def from_partner(block, axis, distance):
    count = lax.axis_size(axis)
    route = []
    for low in range(count):
        high = low | 1 << distance
        if high != low and high < count:
            route += [(low, high), (high, low)]
    return lax.ppermute(block, axis, route)


def dispatch(send_block):
    return lax.all_to_all(send_block, ("node", "local"), split_axis=0, concat_axis=0, tiled=True)


def combine(send_block):
    return lax.all_to_all(send_block, ("node", "local"), split_axis=0, concat_axis=0, tiled=True)


def half_hidden(received, gate_half, up_half, dtype):
    expert_rows = received.reshape(-1, received.shape[-1])
    gate_out = jnp.dot(expert_rows, gate_half, preferred_element_type=jnp.float32)
    up_out = jnp.dot(expert_rows, up_half, preferred_element_type=jnp.float32)
    return (jax.nn.silu(gate_out) * up_out).astype(dtype)


def side_by_side(own_part, other_part, parity, axis):
    lower = jnp.where(parity == 0, own_part, other_part)
    upper = jnp.where(parity == 0, other_part, own_part)
    return jnp.concatenate([lower, upper], axis=axis)


def local(
    tokens,
    expert_ids,
    gate_codes,
    gate_halves,
    up_halves,
    down_halves,
    shared_gate,
    shared_up,
    shared_down,
):
    tok_rows, features = tokens.shape
    fanout = expert_ids.shape[1]
    devices = lax.axis_size("node") * lax.axis_size("local")
    experts = devices // 2
    capacity = 2 * (5 * tok_rows * fanout // (6 * experts) + 1)
    parity = lax.axis_index("local") % 2
    flat_ids = expert_ids.reshape(-1)
    onehot = (flat_ids[:, None] == jnp.arange(experts, dtype=jnp.int32)[None, :]).astype(jnp.int32)
    slot_index = jnp.sum((jnp.cumsum(onehot, axis=0) - 1) * onehot, axis=1)
    dest_row = flat_ids * capacity + slot_index
    owner_row = jnp.arange(tok_rows * fanout, dtype=jnp.int32) // fanout
    buffer = (
        jnp.zeros((experts * capacity, features), tokens.dtype).at[dest_row].set(tokens[owner_row])
    )
    codes = gate_codes.astype(jnp.float32)
    weights = (codes / jnp.sum(codes, axis=1, keepdims=True)).reshape(-1)
    send_block = jnp.broadcast_to(
        buffer.reshape(experts, 1, capacity, features), (experts, 2, capacity, features)
    ).reshape(devices, capacity, features)
    received = dispatch(send_block)
    hidden_own = half_hidden(received, gate_halves[0], up_halves[0], tokens.dtype)
    hidden_other = from_partner(hidden_own, "local", 0)
    hidden = side_by_side(hidden_own, hidden_other, parity, 1)
    result = jnp.dot(hidden, down_halves[0], preferred_element_type=jnp.float32).astype(
        tokens.dtype
    )
    returned = combine(result.reshape(devices, capacity, features // 2))
    outputs = (
        returned.reshape(experts, 2, capacity, features // 2)
        .transpose(0, 2, 1, 3)
        .reshape(experts * capacity, features)
    )
    picked = outputs[dest_row].astype(jnp.float32) * weights[:, None]
    routed = jnp.sum(picked.reshape(tok_rows, fanout, features), axis=1)
    block_rows = lax.all_gather(tokens, "local", axis=0, tiled=True)
    gate_part = jnp.dot(block_rows, shared_gate, preferred_element_type=jnp.float32)
    up_part = jnp.dot(block_rows, shared_up, preferred_element_type=jnp.float32)
    shared_hidden = (jax.nn.silu(gate_part) * up_part).astype(tokens.dtype)
    block_rows = shared_hidden
    shared_out = lax.psum_scatter(
        jnp.dot(block_rows, shared_down, preferred_element_type=jnp.float32).astype(jnp.bfloat16),
        "local",
        scatter_dimension=0,
        tiled=True,
    ).astype(jnp.float32)
    return (routed + shared_out).astype(tokens.dtype)


def place():
    node, chip, core = lax.axis_index("node"), lax.axis_index("chip"), lax.axis_index("core")
    return node // 2, node % 2, chip, core


def near(z, x, y, core, first):
    along_x = 1 - core if first else core
    return (z * 2 + x + along_x * (1 - 2 * x), y + (1 - along_x) * (1 - 2 * y), core)


def slot_of(line, z, x, y, core, p_other, q_other):
    x_other = p_other * (1 - core) + q_other * core
    y_other = p_other * core + q_other * (1 - core)
    return line * (2 * (x + x_other * (1 - 2 * x)) + y + y_other * (1 - 2 * y)) + z


def greet(devices):
    barrier = pltpu.get_barrier_semaphore()
    for device in devices:
        pl.semaphore_signal(barrier, inc=1, device_id=device, device_id_type=MESH)
    pl.semaphore_wait(barrier, len(devices))


def gather_kernel(line, tokens, gathered, own_sem, send_sem, recv_sem):
    z, x, y, core = place()
    p_device, q_device = near(z, x, y, core, True), near(z, x, y, core, False)
    lines = [(lax.rem(z + d, line) * 2 + x, y, core) for d in range(1, line)]
    greet(lines + [p_device, q_device])
    me = slot_of(line, z, x, y, core, 0, 0)

    def push(source, slot, count, device):
        copy = pltpu.make_async_remote_copy(
            src_ref=source,
            dst_ref=gathered.at[slot],
            send_sem=send_sem.at[count],
            recv_sem=recv_sem.at[slot],
            device_id=device,
            device_id_type=MESH,
        )
        copy.start()
        return copy

    def arrived(slot):
        pltpu.make_async_remote_copy(
            src_ref=gathered.at[slot],
            dst_ref=gathered.at[slot],
            send_sem=send_sem.at[0],
            recv_sem=recv_sem.at[slot],
            device_id=q_device,
            device_id_type=MESH,
        ).wait_recv()

    sent = []
    sent.append(push(tokens, me, len(sent), q_device))
    for device in lines:
        sent.append(push(tokens, me, len(sent), device))
    sent.append(push(tokens, me, len(sent), p_device))
    own = pltpu.make_async_copy(tokens, gathered.at[me], own_sem)
    own.start()
    for d in [*range(1, line, 2), *range(2, line, 2)]:
        slot = slot_of(line, lax.rem(z + d, line), x, y, core, 0, 0)
        arrived(slot)
        sent.append(push(gathered.at[slot], slot, len(sent), q_device))
        sent.append(push(gathered.at[slot], slot, len(sent), p_device))
    for d in [0, *range(1, line, 2), *range(2, line, 2)]:
        slot = slot_of(line, lax.rem(z + d, line), x, y, core, 1, 0)
        arrived(slot)
        sent.append(push(gathered.at[slot], slot, len(sent), q_device))
    for p_other in (0, 1):
        for d in range(line):
            arrived(slot_of(line, lax.rem(z + d, line), x, y, core, p_other, 1))
    for copy in sent:
        copy.wait_send()
    own.wait()


def gather_plane(tokens):
    chips = lax.axis_size("node") * lax.axis_size("chip")
    inside = pl.BlockSpec(memory_space=pltpu.VMEM)
    return pl.pallas_call(
        functools.partial(gather_kernel, chips // 4),
        out_shape=jax.ShapeDtypeStruct((chips, *tokens.shape), tokens.dtype),
        in_specs=[inside],
        out_specs=inside,
        scratch_shapes=[
            pltpu.SemaphoreType.DMA,
            pltpu.SemaphoreType.DMA((chips - 1,)),
            pltpu.SemaphoreType.DMA((chips,)),
        ],
        compiler_params=pltpu.CompilerParams(
            collective_id=0, has_side_effects=True, vmem_limit_bytes=16 << 20
        ),
        cost_estimate=pl.CostEstimate(flops=80 << 30, bytes_accessed=128 << 20, transcendentals=0),
    )(tokens)


def reduce_kernel(line, *refs):
    gathered, scale, extra = refs[:3]
    gate, up, down = refs[3:5], refs[5:7], refs[7:9]
    out, terms, from_q, from_p, from_z, send_sem, q_sem, p_sem, z_sem = refs[9:]
    z, x, y, core = place()
    p_device, q_device = near(z, x, y, core, True), near(z, x, y, core, False)
    lines = [(lax.rem(z + d, line) * 2 + x, y, core) for d in range(1, line)]
    greet(lines + [p_device, q_device])
    turn = [*range(1, line), 0]

    def push(source, target, sem, count, device):
        copy = pltpu.make_async_remote_copy(
            src_ref=source,
            dst_ref=target,
            send_sem=send_sem.at[count],
            recv_sem=sem,
            device_id=device,
            device_id_type=MESH,
        )
        copy.start()
        return copy

    def add_up(target, sources):
        def step(i, carry):
            rows = pl.ds(pl.multiple_of(i * 16, 16), 16)
            total = sources[0][rows, :].astype(jnp.float32)
            for source in sources[1:]:
                total = total + source[rows, :].astype(jnp.float32)
            target[rows, :] = total.astype(target.dtype)
            return carry

        lax.fori_loop(0, out.shape[0] // 16, step, 0)

    def serve(p_other, q_other):
        first = slot_of(line, 0, x, y, core, p_other, q_other)
        features = gathered.shape[2]
        rows = gathered[pl.ds(first, line)].reshape(line * gathered.shape[1], features)
        hidden = []
        for half in (0, 1):
            gate_out = lax.dot_general(rows, gate[half][...], NT, preferred_element_type=jnp.float32)
            up_out = lax.dot_general(rows, up[half][...], NT, preferred_element_type=jnp.float32)
            hidden.append((jax.nn.silu(gate_out) * up_out).astype(rows.dtype))
        factor = scale[pl.ds(first, line)].reshape(rows.shape[0], 1)
        width = features // 2
        depth = hidden[0].shape[1]
        own_rows = pl.ds(pl.multiple_of(core * depth, 64), depth)
        other_rows = pl.ds(pl.multiple_of((1 - core) * depth, 64), depth)
        for half in (0, 1):
            result = jnp.dot(hidden[0], down[half][own_rows, :], preferred_element_type=jnp.float32)
            result += jnp.dot(
                hidden[1], down[half][other_rows, :], preferred_element_type=jnp.float32
            )
            terms[pl.ds(first, line), :, half * width : (half + 1) * width] = (
                (result * factor).astype(terms.dtype).reshape(line, -1, width)
            )
        block = first // line

        @pl.when(block // 2 == x)
        def _():
            mine = terms.at[first + z]
            add_up(mine, [mine, extra.at[block % 2]])

    sent, q_copies, p_copies, z_copies = [], {}, {}, {}
    for p_other in (1, 0):
        serve(p_other, 1)
        for d in turn:
            slot = slot_of(line, lax.rem(z + d, line), x, y, core, p_other, 1)
            at = p_other * line + d
            copy = push(terms.at[slot], from_q.at[at], q_sem.at[at], len(sent), q_device)
            sent.append(copy)
            q_copies[p_other, d] = copy
    serve(1, 0)
    for d in turn:
        at = line + d
        slot = slot_of(line, lax.rem(z + d, line), x, y, core, 1, 0)
        q_copies[1, d].wait_recv()
        add_up(terms.at[slot], [terms.at[slot], from_q.at[at]])
        p_copies[d] = push(terms.at[slot], from_p.at[d], p_sem.at[d], len(sent), p_device)
        sent.append(p_copies[d])
    serve(0, 0)
    for d in turn:
        slot = slot_of(line, lax.rem(z + d, line), x, y, core, 0, 0)
        q_copies[0, d].wait_recv()
        p_copies[d].wait_recv()
        sources = [terms.at[slot], from_q.at[d], from_p.at[d]]
        if d:
            add_up(terms.at[slot], sources)
            z_copies[d] = push(
                terms.at[slot], from_z.at[d - 1], z_sem.at[d - 1], len(sent), lines[d - 1]
            )
            sent.append(z_copies[d])
        else:
            for other in range(1, line):
                z_copies[other].wait_recv()
            add_up(out, sources + [from_z.at[other - 1] for other in range(1, line)])
    for copy in sent:
        copy.wait_send()


def reduce_plane(gathered, *operands):
    chips, rows, features = gathered.shape
    line = chips // 4
    inside = pl.BlockSpec(memory_space=pltpu.VMEM)
    return pl.pallas_call(
        functools.partial(reduce_kernel, line),
        out_shape=jax.ShapeDtypeStruct((rows, features), gathered.dtype),
        in_specs=[inside] * (1 + len(operands)),
        out_specs=inside,
        scratch_shapes=[
            pltpu.VMEM((chips, rows, features), gathered.dtype),
            pltpu.VMEM((2 * line, rows, features), gathered.dtype),
            pltpu.VMEM((line, rows, features), gathered.dtype),
            pltpu.VMEM((line - 1, rows, features), gathered.dtype),
            pltpu.SemaphoreType.DMA((chips - 1,)),
            pltpu.SemaphoreType.DMA((2 * line,)),
            pltpu.SemaphoreType.DMA((line,)),
            pltpu.SemaphoreType.DMA((line - 1,)),
        ],
        compiler_params=pltpu.CompilerParams(
            collective_id=1, has_side_effects=True, vmem_limit_bytes=60 << 20
        ),
    )(gathered, *operands)


def gated(rows, gate, up):
    gate_out = jnp.dot(rows, gate, preferred_element_type=jnp.float32)
    up_out = jnp.dot(rows, up, preferred_element_type=jnp.float32)
    return (jax.nn.silu(gate_out) * up_out).astype(rows.dtype)


def dense(
    tokens,
    expert_ids,
    gate_codes,
    gate_halves,
    up_halves,
    down_halves,
    shared_gate,
    shared_up,
    shared_down,
):
    rows, features = tokens.shape
    planes = ("node", "chip")
    chips = lax.axis_size("node") * lax.axis_size("chip")
    group_chips = lax.axis_size("chip")
    core = lax.axis_index("core")
    node = lax.axis_index("node")

    codes = gate_codes.astype(jnp.float32)
    weights = codes / jnp.sum(codes, axis=1, keepdims=True)
    onehot = expert_ids[:, :, None] == jnp.arange(chips, dtype=jnp.int32)[None, None, :]
    table = jnp.sum(jnp.where(onehot, weights[:, :, None], 0.0), axis=1)
    share = lax.all_to_all(
        table.T.reshape(chips, 1, rows), planes, split_axis=0, concat_axis=0, tiled=True
    )
    scale = share.reshape(chips // 4, 4, rows).swapaxes(0, 1).reshape(chips, rows, 1)

    def swapped(block):
        return lax.ppermute(block, "core", [(0, 1), (1, 0)])

    gate, up, down = gate_halves[0].T, up_halves[0].T, down_halves[0]
    s_gate, s_up, s_down = shared_gate.T, shared_up.T, shared_down
    others = [swapped(w) for w in (s_gate, s_up, s_down, gate, up, down)]
    plane_rows = gather_plane(tokens)

    fine = plane_rows.reshape(2, group_chips, chips // 4, rows, features)
    group = lax.dynamic_slice(
        fine, (node % 2, 0, node // 2, 0, 0), (1, group_chips, 1, rows, features)
    ).reshape(group_chips * rows, features)
    shared_part = sum(
        jnp.dot(gated(group, g.T, u.T), w, preferred_element_type=jnp.float32)
        .astype(tokens.dtype)
        .astype(jnp.float32)
        for g, u, w in ((s_gate, s_up, s_down), others[:3])
    )
    extra = shared_part.astype(tokens.dtype).reshape(group_chips, rows, features)
    width = features // 2
    extra = jnp.where(core == 0, extra, jnp.roll(extra, width, axis=2))
    total = reduce_plane(plane_rows, scale, extra, gate, others[3], up, others[4], down, others[5])
    return jnp.where(core == 0, total, jnp.roll(total, width, axis=1))


def program(mesh, row, pieces, body):
    in_specs = (
        P(row, None),
        P(row, None),
        P(row, None),
        P(row, None, None),
        P(row, None, None),
        P(row, None, None),
        P(None, pieces),
        P(None, pieces),
        P(pieces, None),
    )
    return jax.shard_map(
        body, mesh=mesh, in_specs=in_specs, out_specs=P(row, None), check_vma=False
    )


def solution(mesh):
    experts = mesh.devices.size // 2
    fine = jax.sharding.Mesh(
        mesh.devices.reshape(mesh.devices.shape[0], -1, 2), ("node", "chip", "core")
    )

    def run(tokens, expert_ids, *others):
        if mesh.shape["local"] == 4 and experts <= 4 * expert_ids.shape[1]:
            whole = program(fine, ("node", "chip", "core"), ("chip", "core"), dense)
        else:
            whole = program(mesh, ("node", "local"), "local", local)
        return whole(tokens, expert_ids, *others)

    return run
```

```python
import functools

import jax
import jax.numpy as jnp
from jax import lax
from jax.experimental import pallas as pl
from jax.experimental.pallas import tpu as pltpu
from jax.sharding import PartitionSpec as P

MESH = pl.DeviceIdType.MESH
NT = (((1,), (1,)), ((), ()))


def from_partner(block, axis, distance):
    count = lax.axis_size(axis)
    route = []
    for low in range(count):
        high = low | 1 << distance
        if high != low and high < count:
            route += [(low, high), (high, low)]
    return lax.ppermute(block, axis, route)


def dispatch(send_block):
    return lax.all_to_all(send_block, ("node", "local"), split_axis=0, concat_axis=0, tiled=True)


def combine(send_block):
    return lax.all_to_all(send_block, ("node", "local"), split_axis=0, concat_axis=0, tiled=True)


def half_hidden(received, gate_half, up_half, dtype):
    expert_rows = received.reshape(-1, received.shape[-1])
    gate_out = jnp.dot(expert_rows, gate_half, preferred_element_type=jnp.float32)
    up_out = jnp.dot(expert_rows, up_half, preferred_element_type=jnp.float32)
    return (jax.nn.silu(gate_out) * up_out).astype(dtype)


def side_by_side(own_part, other_part, parity, axis):
    lower = jnp.where(parity == 0, own_part, other_part)
    upper = jnp.where(parity == 0, other_part, own_part)
    return jnp.concatenate([lower, upper], axis=axis)


def local(
    tokens,
    expert_ids,
    gate_codes,
    gate_halves,
    up_halves,
    down_halves,
    shared_gate,
    shared_up,
    shared_down,
):
    tok_rows, features = tokens.shape
    fanout = expert_ids.shape[1]
    devices = lax.axis_size("node") * lax.axis_size("local")
    experts = devices // 2
    capacity = 2 * (5 * tok_rows * fanout // (6 * experts) + 1)
    parity = lax.axis_index("local") % 2
    flat_ids = expert_ids.reshape(-1)
    onehot = (flat_ids[:, None] == jnp.arange(experts, dtype=jnp.int32)[None, :]).astype(jnp.int32)
    slot_index = jnp.sum((jnp.cumsum(onehot, axis=0) - 1) * onehot, axis=1)
    dest_row = flat_ids * capacity + slot_index
    owner_row = jnp.arange(tok_rows * fanout, dtype=jnp.int32) // fanout
    buffer = (
        jnp.zeros((experts * capacity, features), tokens.dtype).at[dest_row].set(tokens[owner_row])
    )
    codes = gate_codes.astype(jnp.float32)
    weights = (codes / jnp.sum(codes, axis=1, keepdims=True)).reshape(-1)
    send_block = jnp.broadcast_to(
        buffer.reshape(experts, 1, capacity, features), (experts, 2, capacity, features)
    ).reshape(devices, capacity, features)
    received = dispatch(send_block)
    hidden_own = half_hidden(received, gate_halves[0], up_halves[0], tokens.dtype)
    hidden_other = from_partner(hidden_own, "local", 0)
    hidden = side_by_side(hidden_own, hidden_other, parity, 1)
    result = jnp.dot(hidden, down_halves[0], preferred_element_type=jnp.float32).astype(
        tokens.dtype
    )
    returned = combine(result.reshape(devices, capacity, features // 2))
    outputs = (
        returned.reshape(experts, 2, capacity, features // 2)
        .transpose(0, 2, 1, 3)
        .reshape(experts * capacity, features)
    )
    picked = outputs[dest_row].astype(jnp.float32) * weights[:, None]
    routed = jnp.sum(picked.reshape(tok_rows, fanout, features), axis=1)
    block_rows = lax.all_gather(tokens, "local", axis=0, tiled=True)
    gate_part = jnp.dot(block_rows, shared_gate, preferred_element_type=jnp.float32)
    up_part = jnp.dot(block_rows, shared_up, preferred_element_type=jnp.float32)
    shared_hidden = (jax.nn.silu(gate_part) * up_part).astype(tokens.dtype)
    block_rows = shared_hidden
    shared_out = lax.psum_scatter(
        jnp.dot(block_rows, shared_down, preferred_element_type=jnp.float32).astype(jnp.bfloat16),
        "local",
        scatter_dimension=0,
        tiled=True,
    ).astype(jnp.float32)
    return (routed + shared_out).astype(tokens.dtype)


def place():
    node, chip, core = lax.axis_index("node"), lax.axis_index("chip"), lax.axis_index("core")
    return node // 2, node % 2, chip, core


def near(z, x, y, core, first):
    along_x = 1 - core if first else core
    return (z * 2 + x + along_x * (1 - 2 * x), y + (1 - along_x) * (1 - 2 * y), core)


def slot_of(line, z, x, y, core, p_other, q_other):
    x_other = p_other * (1 - core) + q_other * core
    y_other = p_other * core + q_other * (1 - core)
    return line * (2 * (x + x_other * (1 - 2 * x)) + y + y_other * (1 - 2 * y)) + z


def greet(devices):
    barrier = pltpu.get_barrier_semaphore()
    for device in devices:
        pl.semaphore_signal(barrier, inc=1, device_id=device, device_id_type=MESH)
    pl.semaphore_wait(barrier, len(devices))


def gather_kernel(line, *refs):
    tokens, s_gate, s_up, s_down, gathered, extra, pair_in, pair_out, pair_back = refs[:9]
    own_sem, send_sem, recv_sem, pair_send, pair_recv = refs[9:]
    z, x, y, core = place()
    p_device, q_device = near(z, x, y, core, True), near(z, x, y, core, False)
    lines = [(lax.rem(z + d, line) * 2 + x, y, core) for d in range(1, line)]
    partner = (z * 2 + x, y, 1 - core)
    greet(lines + [p_device, q_device, partner])
    me = slot_of(line, z, x, y, core, 0, 0)

    def push(source, slot, count, device):
        copy = pltpu.make_async_remote_copy(
            src_ref=source,
            dst_ref=gathered.at[slot],
            send_sem=send_sem.at[count],
            recv_sem=recv_sem.at[slot],
            device_id=device,
            device_id_type=MESH,
        )
        copy.start()
        return copy

    def arrived(slot):
        pltpu.make_async_remote_copy(
            src_ref=gathered.at[slot],
            dst_ref=gathered.at[slot],
            send_sem=send_sem.at[0],
            recv_sem=recv_sem.at[slot],
            device_id=q_device,
            device_id_type=MESH,
        ).wait_recv()

    sent = []
    sent.append(push(tokens, me, len(sent), q_device))
    for device in lines:
        sent.append(push(tokens, me, len(sent), device))
    sent.append(push(tokens, me, len(sent), p_device))
    own = pltpu.make_async_copy(tokens, gathered.at[me], own_sem)
    own.start()

    def to_partner(source, target, at):
        copy = pltpu.make_async_remote_copy(
            src_ref=source,
            dst_ref=target,
            send_sem=pair_send.at[at],
            recv_sem=pair_recv.at[at],
            device_id=partner,
            device_id_type=MESH,
        )
        copy.start()
        return copy

    def shared(rows):
        gate_out = lax.dot_general(rows, s_gate[...], NT, preferred_element_type=jnp.float32)
        up_out = lax.dot_general(rows, s_up[...], NT, preferred_element_type=jnp.float32)
        hidden = (jax.nn.silu(gate_out) * up_out).astype(rows.dtype)
        part = jnp.dot(hidden, s_down[...], preferred_element_type=jnp.float32)
        return part.astype(rows.dtype).reshape(extra.shape)

    pair = [to_partner(tokens, pair_in.at[y], 0)]
    for d in [*range(1, line, 2), *range(2, line, 2)]:
        slot = slot_of(line, lax.rem(z + d, line), x, y, core, 0, 0)
        arrived(slot)
        sent.append(push(gathered.at[slot], slot, len(sent), q_device))
        sent.append(push(gathered.at[slot], slot, len(sent), p_device))
    for d in [0, *range(1, line, 2), *range(2, line, 2)]:
        slot = slot_of(line, lax.rem(z + d, line), x, y, core, 1, 0)
        arrived(slot)
        sent.append(push(gathered.at[slot], slot, len(sent), q_device))
    own.wait()
    arrived(slot_of(line, z, x, y, core, 0, 1))
    beside = line * (2 * x + 1 - y) + z
    pair.append(to_partner(gathered.at[beside], pair_in.at[1 - y], 1))
    for copy in pair:
        copy.wait_recv()
    pair_rows = extra.shape[0] * extra.shape[1]
    pair_out[...] = shared(pair_in[...].reshape(pair_rows, extra.shape[2]))
    pair.append(to_partner(pair_out, pair_back, 2))
    group = [gathered[line * (2 * x + b) + z] for b in (0, 1)]
    extra[...] = shared(jnp.concatenate(group, axis=0))
    pair[2].wait_recv()
    total = extra[...].astype(jnp.float32) + pair_back[...].astype(jnp.float32)
    extra[...] = total.astype(extra.dtype)
    for p_other in (0, 1):
        for d in range(1 - p_other, line):
            arrived(slot_of(line, lax.rem(z + d, line), x, y, core, p_other, 1))
    for copy in sent:
        copy.wait_send()
    for copy in pair:
        copy.wait_send()


def gather_plane(tokens, *shared_weights):
    chips = lax.axis_size("node") * lax.axis_size("chip")
    inside = pl.BlockSpec(memory_space=pltpu.VMEM)
    return pl.pallas_call(
        functools.partial(gather_kernel, chips // 4),
        out_shape=[
            jax.ShapeDtypeStruct((chips, *tokens.shape), tokens.dtype),
            jax.ShapeDtypeStruct((2, *tokens.shape), tokens.dtype),
        ],
        in_specs=[inside] * (1 + len(shared_weights)),
        out_specs=[inside, inside],
        scratch_shapes=[
            pltpu.VMEM((2, *tokens.shape), tokens.dtype),
            pltpu.VMEM((2, *tokens.shape), tokens.dtype),
            pltpu.VMEM((2, *tokens.shape), tokens.dtype),
            pltpu.SemaphoreType.DMA,
            pltpu.SemaphoreType.DMA((chips - 1,)),
            pltpu.SemaphoreType.DMA((chips,)),
            pltpu.SemaphoreType.DMA((3,)),
            pltpu.SemaphoreType.DMA((3,)),
        ],
        compiler_params=pltpu.CompilerParams(
            collective_id=0, has_side_effects=True, vmem_limit_bytes=40 << 20
        ),
        cost_estimate=pl.CostEstimate(flops=80 << 30, bytes_accessed=128 << 20, transcendentals=0),
    )(tokens, *shared_weights)


def reduce_kernel(line, *refs):
    gathered, scale, extra = refs[:3]
    gate, up, down = refs[3:5], refs[5:7], refs[7:9]
    out, terms, from_q, from_p, from_z, send_sem, q_sem, p_sem, z_sem = refs[9:]
    z, x, y, core = place()
    p_device, q_device = near(z, x, y, core, True), near(z, x, y, core, False)
    lines = [(lax.rem(z + d, line) * 2 + x, y, core) for d in range(1, line)]
    greet(lines + [p_device, q_device])
    turn = [*range(1, line), 0]

    def push(source, target, sem, count, device):
        copy = pltpu.make_async_remote_copy(
            src_ref=source,
            dst_ref=target,
            send_sem=send_sem.at[count],
            recv_sem=sem,
            device_id=device,
            device_id_type=MESH,
        )
        copy.start()
        return copy

    def add_up(target, sources):
        def step(i, carry):
            rows = pl.ds(pl.multiple_of(i * 16, 16), 16)
            total = sources[0][rows, :].astype(jnp.float32)
            for source in sources[1:]:
                total = total + source[rows, :].astype(jnp.float32)
            target[rows, :] = total.astype(target.dtype)
            return carry

        lax.fori_loop(0, out.shape[0] // 16, step, 0)

    def serve(p_other, q_other):
        first = slot_of(line, 0, x, y, core, p_other, q_other)
        features = gathered.shape[2]
        rows = gathered[pl.ds(first, line)].reshape(line * gathered.shape[1], features)
        hidden = []
        for half in (0, 1):
            gate_out = lax.dot_general(rows, gate[half][...], NT, preferred_element_type=jnp.float32)
            up_out = lax.dot_general(rows, up[half][...], NT, preferred_element_type=jnp.float32)
            hidden.append((jax.nn.silu(gate_out) * up_out).astype(rows.dtype))
        factor = scale[pl.ds(first, line)].reshape(rows.shape[0], 1)
        width = features // 2
        depth = hidden[0].shape[1]
        own_rows = pl.ds(pl.multiple_of(core * depth, 64), depth)
        other_rows = pl.ds(pl.multiple_of((1 - core) * depth, 64), depth)
        for half in (0, 1):
            result = jnp.dot(hidden[0], down[half][own_rows, :], preferred_element_type=jnp.float32)
            result += jnp.dot(
                hidden[1], down[half][other_rows, :], preferred_element_type=jnp.float32
            )
            terms[pl.ds(first, line), :, half * width : (half + 1) * width] = (
                (result * factor).astype(terms.dtype).reshape(line, -1, width)
            )
        block = first // line

        @pl.when(block // 2 == x)
        def _():
            mine = terms.at[first + z]
            add_up(mine, [mine, extra.at[block % 2]])

    sent, q_copies, p_copies, z_copies = [], {}, {}, {}
    for p_other in (1, 0):
        serve(p_other, 1)
        for d in turn:
            slot = slot_of(line, lax.rem(z + d, line), x, y, core, p_other, 1)
            at = p_other * line + d
            copy = push(terms.at[slot], from_q.at[at], q_sem.at[at], len(sent), q_device)
            sent.append(copy)
            q_copies[p_other, d] = copy
    serve(1, 0)
    for d in turn:
        at = line + d
        slot = slot_of(line, lax.rem(z + d, line), x, y, core, 1, 0)
        q_copies[1, d].wait_recv()
        add_up(terms.at[slot], [terms.at[slot], from_q.at[at]])
        p_copies[d] = push(terms.at[slot], from_p.at[d], p_sem.at[d], len(sent), p_device)
        sent.append(p_copies[d])
    serve(0, 0)
    for d in turn:
        slot = slot_of(line, lax.rem(z + d, line), x, y, core, 0, 0)
        q_copies[0, d].wait_recv()
        p_copies[d].wait_recv()
        sources = [terms.at[slot], from_q.at[d], from_p.at[d]]
        if d:
            add_up(terms.at[slot], sources)
            z_copies[d] = push(
                terms.at[slot], from_z.at[d - 1], z_sem.at[d - 1], len(sent), lines[d - 1]
            )
            sent.append(z_copies[d])
        else:
            for other in range(1, line):
                z_copies[other].wait_recv()
            add_up(out, sources + [from_z.at[other - 1] for other in range(1, line)])
    for copy in sent:
        copy.wait_send()


def reduce_plane(gathered, *operands):
    chips, rows, features = gathered.shape
    line = chips // 4
    inside = pl.BlockSpec(memory_space=pltpu.VMEM)
    return pl.pallas_call(
        functools.partial(reduce_kernel, line),
        out_shape=jax.ShapeDtypeStruct((rows, features), gathered.dtype),
        in_specs=[inside] * (1 + len(operands)),
        out_specs=inside,
        scratch_shapes=[
            pltpu.VMEM((chips, rows, features), gathered.dtype),
            pltpu.VMEM((2 * line, rows, features), gathered.dtype),
            pltpu.VMEM((line, rows, features), gathered.dtype),
            pltpu.VMEM((line - 1, rows, features), gathered.dtype),
            pltpu.SemaphoreType.DMA((chips - 1,)),
            pltpu.SemaphoreType.DMA((2 * line,)),
            pltpu.SemaphoreType.DMA((line,)),
            pltpu.SemaphoreType.DMA((line - 1,)),
        ],
        compiler_params=pltpu.CompilerParams(
            collective_id=1, has_side_effects=True, vmem_limit_bytes=60 << 20
        ),
    )(gathered, *operands)


def dense(
    tokens,
    expert_ids,
    gate_codes,
    gate_halves,
    up_halves,
    down_halves,
    shared_gate,
    shared_up,
    shared_down,
):
    rows, features = tokens.shape
    planes = ("node", "chip")
    chips = lax.axis_size("node") * lax.axis_size("chip")
    core = lax.axis_index("core")

    codes = gate_codes.astype(jnp.float32)
    weights = codes / jnp.sum(codes, axis=1, keepdims=True)
    onehot = expert_ids[:, :, None] == jnp.arange(chips, dtype=jnp.int32)[None, None, :]
    table = jnp.sum(jnp.where(onehot, weights[:, :, None], 0.0), axis=1)
    share = lax.all_to_all(
        table.T.reshape(chips, 1, rows), planes, split_axis=0, concat_axis=0, tiled=True
    )
    scale = share.reshape(chips // 4, 4, rows).swapaxes(0, 1).reshape(chips, rows, 1)

    def swapped(block):
        return lax.ppermute(block, "core", [(0, 1), (1, 0)])

    gate, up, down = gate_halves[0].T, up_halves[0].T, down_halves[0]
    others = [swapped(w) for w in (gate, up, down)]
    plane_rows, extra = gather_plane(tokens, shared_gate.T, shared_up.T, shared_down)
    width = features // 2
    extra = jnp.where(core == 0, extra, jnp.roll(extra, width, axis=2))
    total = reduce_plane(plane_rows, scale, extra, gate, others[0], up, others[1], down, others[2])
    return jnp.where(core == 0, total, jnp.roll(total, width, axis=1))


def program(mesh, row, pieces, body):
    in_specs = (
        P(row, None),
        P(row, None),
        P(row, None),
        P(row, None, None),
        P(row, None, None),
        P(row, None, None),
        P(None, pieces),
        P(None, pieces),
        P(pieces, None),
    )
    return jax.shard_map(
        body, mesh=mesh, in_specs=in_specs, out_specs=P(row, None), check_vma=False
    )


def solution(mesh):
    experts = mesh.devices.size // 2
    fine = jax.sharding.Mesh(
        mesh.devices.reshape(mesh.devices.shape[0], -1, 2), ("node", "chip", "core")
    )

    def run(tokens, expert_ids, *others):
        if mesh.shape["local"] == 4 and experts <= 4 * expert_ids.shape[1]:
            whole = program(fine, ("node", "chip", "core"), ("chip", "core"), dense)
        else:
            whole = program(mesh, ("node", "local"), "local", local)
        return whole(tokens, expert_ids, *others)

    return run
```
